256 devices in a mesh: ctx: 32 (over x, y, core), head: 8 (over z).
Axes of the slice: x: 4, y: 4, z: 8, core: 2. Of those that a mesh axis runs over, the one named last changes fastest.
Arguments:
- query_proj: bfloat16 [16384, 2048], P('ctx', 'head'), may hold values from -32 to 32
- projected_keys: bfloat16 [16384, 1024], P('ctx', 'head'), may hold values from -32 to 32
- projected_values: bfloat16 [16384, 1024], P('ctx', 'head'), may hold values from -12 to 12
- w_out: bfloat16 [2048, 4096], P('head'), may hold values from -0.1875 to 0.1875
- attended_blocks: int32 [32, 12], replicated, may hold values from -1 to 31, as said below
- grad_out: bfloat16 [16384, 4096], P('ctx', 'head'), may hold values from -6 to 6
Outputs:
- layer_out: bfloat16 [16384, 4096], P('ctx', 'head')
- grad_query: float32 [16384, 2048], P('ctx', 'head')
- grad_key: float32 [16384, 1024], P('ctx', 'head')
- grad_value: float32 [16384, 1024], P('ctx', 'head')
- grad_wout: float32 [2048, 4096], P('head', 'ctx')
The draws below stay inside these ranges and needn't reach their ends.
Inputs may be any that keep to these rules, and one draw needn't show every extreme that they name: `attended_blocks`: row b lists key blocks: its first entry is b; if b >= 16 its second entry is b - 16; the other live entries are distinct blocks among b - 11 to b - 1; -1 fills the unused entries. Row b has between min(2, b + 1) and 12 live entries, and some row has exactly 12.
All inputs are finite; a program needn't handle non-finite values.
Results may differ from the reference program's by a relative error of at most 0.04.
Values may be sent and summed in bfloat16 or wider, within the bound.
No kernel may reach another device: no remote copies, remote signals or barrier semaphores. Data moves between devices by JAX's collectives and lax.ppermute only.
A program may use at most 128 MiB of HBM per device.

```python
import jax
import jax.numpy as jnp
from jax import lax

D = 4096
QUERY_HEADS = 16
KEY_VALUE_HEADS = 8
HEAD_SIZE = 128
BLOCK_TOKENS = 512
BLK_DEV = 1
SEGMENT_BLOCKS = 32
SEGMENT_TOKENS = 16384
LIST = 12
N_CTX = 32
N_HEAD = 8


def drawn(key):
    base_key = jax.random.fold_in(key, 907)
    query_key, random_keys_seed = jax.random.split(base_key, 2)
    query_matrix = 2.0 * jax.random.truncated_normal(query_key, -3.0, 3.0, (SEGMENT_TOKENS, QUERY_HEADS * HEAD_SIZE), jnp.float32)
    returned_keys = jax.random.truncated_normal(random_keys_seed, -4.0, 4.0, (SEGMENT_TOKENS, KEY_VALUE_HEADS * HEAD_SIZE), jnp.float32)
    return (query_matrix, returned_keys)


def draw_query_proj(key, part):
    return drawn(key)[0].astype(jnp.bfloat16)


def draw_projected_keys(key, part):
    return drawn(key)[1].astype(jnp.bfloat16)


def draw_attended_blocks(key, part):
    base_key = jax.random.fold_in(key, 311)
    first_key, second_key, force_key, score_key = jax.random.split(base_key, 4)
    first_draw = jax.random.randint(first_key, (SEGMENT_BLOCKS,), 0, 11)
    second_draw = jax.random.randint(second_key, (SEGMENT_BLOCKS,), 0, 11)
    wanted = 2 + first_draw * second_draw // 10
    blocks = jnp.arange(SEGMENT_BLOCKS, dtype=jnp.int32)
    forced = jax.random.randint(force_key, (), LIST - 1, SEGMENT_BLOCKS)
    wanted = jnp.where(blocks == forced, LIST, wanted)
    lengths = jnp.minimum(jnp.minimum(wanted, LIST), blocks + 1)
    far_block = blocks - SEGMENT_BLOCKS // 2
    has_far = far_block >= 0
    raw_scores = jax.random.randint(score_key, (SEGMENT_BLOCKS, SEGMENT_BLOCKS), 0, 1 << 20)
    excluded = (blocks[None, :] >= blocks[:, None]) | (blocks[None, :] < blocks[:, None] - (LIST - 1)) | (blocks[None, :] == far_block[:, None])
    ranked = jnp.where(excluded, -1, raw_scores * SEGMENT_BLOCKS + blocks[None, :])
    picked_scores, chosen = lax.top_k(ranked, LIST - 1)
    chosen = chosen.astype(jnp.int32)
    with_far = jnp.concatenate([far_block[:, None], chosen[:, :LIST - 2]], 1)
    candidates = jnp.where(has_far[:, None], with_far, chosen)
    slot_ids = jnp.arange(LIST - 1, dtype=jnp.int32)[None, :]
    earlier = jnp.where(slot_ids < (lengths - 1)[:, None], candidates, -1)
    return jnp.concatenate([blocks[:, None], earlier], 1).astype(jnp.int32)


def raised(entries, key, source, target, blocks, factor):
    def block_of(axis_at):
        return (jnp.arange(entries.shape[axis_at]) // (entries.shape[axis_at] // blocks)).reshape((-1,) + (1,) * (entries.ndim - 1 - axis_at))

    near = jax.random.permutation(key, blocks)[block_of(target)]
    other_side = (block_of(target) + blocks // 2) % blocks
    return jnp.where((block_of(source) == near) | (block_of(source) == other_side), factor * entries, entries)


def level_of(own_key, dims, cuts, low, top_value):
    level = 1.0
    for dim, parts in cuts:
        steps = jax.random.uniform(jax.random.fold_in(jax.random.fold_in(own_key, 6), dim), (parts,), jnp.float32, low / len(cuts), top_value / len(cuts))
        level = level * jnp.repeat(jnp.exp(steps), dims[dim] // parts).reshape((-1,) + (1,) * (len(dims) - 1 - dim))
    return level


def gaussian(own_key, dims, scale, reach, shards=(), kind=jnp.bfloat16):
    drawn = jax.random.normal(own_key, dims, jnp.float32) * scale
    if len(shards) > 0:
        drawn = level_of(own_key, dims, shards, -0.22, 0.18) * drawn
    return jnp.clip(drawn, min=-reach, max=reach).astype(kind)


def heavy_noise(own_key, extent, spread, bound, cuts, heavy, kind=jnp.bfloat16):
    values = spread * jax.random.normal(own_key, extent, jnp.float32)
    if cuts:
        values = values * level_of(own_key, extent, cuts, -0.22, 0.18)
    return jnp.clip(raised(values, jax.random.fold_in(own_key, 3), *heavy), -bound, bound).astype(kind)


def setup_inputs(seed: int = 0) -> dict:
    keys = jax.random.split(jax.random.key(seed), 7)
    query_proj = draw_query_proj(jax.random.fold_in(keys[6], 71), 0)
    projected_keys = draw_projected_keys(jax.random.fold_in(keys[6], 71), 0)
    projected_values = gaussian(keys[2], (SEGMENT_TOKENS, KEY_VALUE_HEADS * HEAD_SIZE), 2.0, 12.0, ((0, 32), (1, 8)))
    w_out = heavy_noise(keys[3], (QUERY_HEADS * HEAD_SIZE, D), (QUERY_HEADS * HEAD_SIZE) ** -0.5, 0.1875, ((0, 8),), (0, 1, 8, 2.0))
    attended_blocks = draw_attended_blocks(jax.random.fold_in(keys[6], 71), 0)
    grad_out = heavy_noise(keys[5], (SEGMENT_TOKENS, D), 1.0, 6.0, ((0, 32), (1, 8)), (0, 1, 32, 2.75))
    return {"query_proj": query_proj, "projected_keys": projected_keys, "projected_values": projected_values, "w_out": w_out, "attended_blocks": attended_blocks, "grad_out": grad_out}


def load_key_block(source, key_block_index, kv_heads):
    rows_per_block = lax.dynamic_slice_in_dim(source, key_block_index * BLOCK_TOKENS, BLOCK_TOKENS, 0)
    return rows_per_block.reshape(BLOCK_TOKENS, kv_heads, HEAD_SIZE).astype(jnp.float32)


def causal_scores(query_portion, key_row_slice, key_block_index, diagonal_block):
    raw_scores = jnp.einsum('ikgd,jkd->kgij', query_portion, key_row_slice) * (HEAD_SIZE ** -0.5)
    row_pos = lax.broadcasted_iota(jnp.int32, (BLOCK_TOKENS, BLOCK_TOKENS), 0)
    col_pos = lax.broadcasted_iota(jnp.int32, (BLOCK_TOKENS, BLOCK_TOKENS), 1)
    allowed = (key_block_index < diagonal_block) | (col_pos <= row_pos)
    return jnp.where(allowed, raw_scores, -jnp.inf)


def rounded(values):
    low_values = lax.optimization_barrier(values.astype(jnp.bfloat16))
    return low_values.astype(jnp.float32)


def reference(query_proj, projected_keys, projected_values, w_out, attended_blocks, grad_out):
    heads_per_group = QUERY_HEADS // KEY_VALUE_HEADS
    slot_count = attended_blocks.shape[1]
    score_scale = HEAD_SIZE ** -0.5
    head_cols = QUERY_HEADS * HEAD_SIZE // N_HEAD
    range_rows = SEGMENT_TOKENS // N_CTX
    key_column_span = KEY_VALUE_HEADS * HEAD_SIZE

    def heads_of(source, diagonal_block):
        rows_per_block = lax.dynamic_slice_in_dim(source, diagonal_block * BLOCK_TOKENS, BLOCK_TOKENS, 0)
        return rows_per_block.reshape(BLOCK_TOKENS, KEY_VALUE_HEADS, heads_per_group, HEAD_SIZE).astype(jnp.float32)

    def forward_block(diagonal_block):
        listed = attended_blocks[diagonal_block]
        query_portion = heads_of(query_proj, diagonal_block)

        def opening_sweep(slot_num, running):
            key_block_index = listed[slot_num]

            def live(present_block):
                running_largest, softmax_denominator = present_block
                score_matrix = causal_scores(query_portion, load_key_block(projected_keys, key_block_index, KEY_VALUE_HEADS), key_block_index, diagonal_block)
                new_largest = jnp.maximum(running_largest, jnp.max(score_matrix, -1))
                softmax_denominator = softmax_denominator * jnp.exp(running_largest - new_largest) + jnp.sum(jnp.exp(score_matrix - new_largest[..., None]), -1)
                return new_largest, softmax_denominator

            return lax.cond(key_block_index >= 0, live, lambda present_block: present_block, running)

        initial_state = (jnp.full((KEY_VALUE_HEADS, heads_per_group, BLOCK_TOKENS), -jnp.inf, jnp.float32), jnp.zeros((KEY_VALUE_HEADS, heads_per_group, BLOCK_TOKENS), jnp.float32))
        running_largest, softmax_denominator = lax.fori_loop(0, slot_count, opening_sweep, initial_state)

        def closing_sweep(slot_num, weighted_values):
            key_block_index = listed[slot_num]

            def live(present_block):
                score_matrix = causal_scores(query_portion, load_key_block(projected_keys, key_block_index, KEY_VALUE_HEADS), key_block_index, diagonal_block)
                attention_weights = rounded(jnp.exp(score_matrix - running_largest[..., None]))
                return present_block + jnp.einsum('mayf,fmb->mayb', attention_weights, load_key_block(projected_values, key_block_index, KEY_VALUE_HEADS))

            return lax.cond(key_block_index >= 0, live, lambda present_block: present_block, weighted_values)

        weighted_values = lax.fori_loop(0, slot_count, closing_sweep, jnp.zeros((KEY_VALUE_HEADS, heads_per_group, BLOCK_TOKENS, HEAD_SIZE), jnp.float32))
        attn_block = (weighted_values / softmax_denominator[..., None]).astype(jnp.bfloat16)
        attn_block = attn_block.transpose(2, 0, 1, 3).reshape(BLOCK_TOKENS, QUERY_HEADS * HEAD_SIZE)
        return attn_block, running_largest + jnp.log(softmax_denominator)

    attn_blocks, log_totals = lax.map(forward_block, jnp.arange(SEGMENT_BLOCKS, dtype=jnp.int32))
    attention = attn_blocks.reshape(SEGMENT_TOKENS, QUERY_HEADS * HEAD_SIZE)

    def add_group(out_sum, group_index):
        column_part = lax.dynamic_slice_in_dim(attention, group_index * head_cols, head_cols, 1)
        row_part = lax.dynamic_slice_in_dim(w_out, group_index * head_cols, head_cols, 0)
        return out_sum + rounded(jnp.dot(column_part, row_part, preferred_element_type=jnp.float32)), None

    out_sum, unused = lax.scan(add_group, jnp.zeros((SEGMENT_TOKENS, D), jnp.float32), jnp.arange(N_HEAD, dtype=jnp.int32))
    layer_out = out_sum.astype(jnp.bfloat16)

    grad_attn = jnp.dot(grad_out, w_out.T, preferred_element_type=jnp.float32).astype(jnp.bfloat16)

    def add_range(weight_sum, range_index):
        attn_rows = lax.dynamic_slice_in_dim(attention, range_index * range_rows, range_rows, 0)
        grad_rows = lax.dynamic_slice_in_dim(grad_out, range_index * range_rows, range_rows, 0)
        term = lax.dot_general(attn_rows, grad_rows, (((0,), (0,)), ((), ())), preferred_element_type=jnp.float32)
        return weight_sum + rounded(term), None

    grad_wout, unused = lax.scan(add_range, jnp.zeros((QUERY_HEADS * HEAD_SIZE, D), jnp.float32), jnp.arange(N_CTX, dtype=jnp.int32))

    def backward_block(diagonal_block, key_part, value_part):
        listed = attended_blocks[diagonal_block]
        query_portion = heads_of(query_proj, diagonal_block)
        grad_heads = heads_of(grad_attn, diagonal_block)
        attn_heads = heads_of(attention, diagonal_block)
        delta = jnp.einsum('ikgd,ikgd->kgi', grad_heads, attn_heads)
        log_total = log_totals[diagonal_block]

        def forward_visit(slot_num, running):
            key_block_index = listed[slot_num]

            def live(present_block):
                query_gradient_total, key_increments, value_increments = present_block
                key_row_slice = load_key_block(projected_keys, key_block_index, KEY_VALUE_HEADS)
                value_row_slice = load_key_block(projected_values, key_block_index, KEY_VALUE_HEADS)
                score_matrix = causal_scores(query_portion, key_row_slice, key_block_index, diagonal_block)
                probs = jnp.exp(score_matrix - log_total[..., None])
                grad_probs = jnp.einsum('ikgd,jkd->kgij', grad_heads, value_row_slice)
                grad_scores = rounded(score_scale * probs * (grad_probs - delta[..., None]))
                query_gradient_total = query_gradient_total + jnp.einsum('mayf,fmb->mayb', grad_scores, key_row_slice)
                key_add = jnp.einsum('kgij,ikgd->jkd', grad_scores, query_portion).reshape(BLOCK_TOKENS, key_column_span)
                value_add = jnp.einsum('kgij,ikgd->jkd', rounded(probs), grad_heads).reshape(BLOCK_TOKENS, key_column_span)
                key_increments = lax.dynamic_update_index_in_dim(key_increments, key_add, slot_num, 0)
                value_increments = lax.dynamic_update_index_in_dim(value_increments, value_add, slot_num, 0)
                return query_gradient_total, key_increments, value_increments

            return lax.cond(key_block_index >= 0, live, lambda present_block: present_block, running)

        initial_state = (jnp.zeros((KEY_VALUE_HEADS, heads_per_group, BLOCK_TOKENS, HEAD_SIZE), jnp.float32), jnp.zeros((slot_count, BLOCK_TOKENS, key_column_span), jnp.float32), jnp.zeros((slot_count, BLOCK_TOKENS, key_column_span), jnp.float32))
        query_gradient_total, key_increments, value_increments = lax.fori_loop(0, slot_count, forward_visit, initial_state)
        target_blocks = jnp.where(listed >= 0, listed, diagonal_block).astype(jnp.int32)
        key_part = key_part.reshape(SEGMENT_BLOCKS, BLOCK_TOKENS, key_column_span).at[target_blocks].add(key_increments).reshape(SEGMENT_TOKENS, key_column_span)
        value_part = value_part.reshape(SEGMENT_BLOCKS, BLOCK_TOKENS, key_column_span).at[target_blocks].add(value_increments).reshape(SEGMENT_TOKENS, key_column_span)
        return query_gradient_total.transpose(2, 0, 1, 3).reshape(BLOCK_TOKENS, QUERY_HEADS * HEAD_SIZE), key_part, value_part

    def range_grads(totals, range_index):
        key_part = jnp.zeros((SEGMENT_TOKENS, key_column_span), jnp.float32)
        value_part = jnp.zeros((SEGMENT_TOKENS, key_column_span), jnp.float32)
        query_rows = []
        for local_block in range(BLK_DEV):
            diagonal_block = (range_index * BLK_DEV + local_block).astype(jnp.int32)
            query_block, key_part, value_part = backward_block(diagonal_block, key_part, value_part)
            query_rows.append(query_block)
        return (totals[0] + rounded(key_part), totals[1] + rounded(value_part)), jnp.concatenate(query_rows, 0)

    start_totals = (jnp.zeros((SEGMENT_TOKENS, key_column_span), jnp.float32), jnp.zeros((SEGMENT_TOKENS, key_column_span), jnp.float32))
    totals, query_ranges = lax.scan(range_grads, start_totals, jnp.arange(N_CTX, dtype=jnp.int32))
    grad_query = query_ranges.reshape(SEGMENT_TOKENS, QUERY_HEADS * HEAD_SIZE)
    return (layer_out, grad_query, totals[0], totals[1], grad_wout)
```

```python
import functools

import jax
import jax.numpy as jnp
from jax import lax
from jax.experimental import pallas as pl
from jax.experimental.pallas import tpu as pltpu
from jax.sharding import PartitionSpec as P

HEAD_SIZE = 128
BT = 512
NB = 32
SCALE = HEAD_SIZE**-0.5
LOG2E = 1.4426950408889634
C2 = SCALE * LOG2E
ROWS = 256
F32 = jnp.float32
BF16 = jnp.bfloat16


def dot_t(a, b):
    return lax.dot_general(a, b, (((1,), (1,)), ((), ())), preferred_element_type=F32)


def fwd_body(n, diag, first, last, *refs):
    flags, q_ref = refs[0], refs[1]
    pos = 2
    if not first:
        m_in, l_in, acc_in = refs[pos : pos + 3]
        pos += 3
    entries = refs[pos : pos + n]
    pos += n
    if last:
        attn_ref, lse_ref = refs[pos : pos + 2]
        pos += 2
        m_ref, l_ref, acc_ref = refs[pos : pos + 3]
        pos += 3
    else:
        m_ref, l_ref, acc_ref = refs[pos : pos + 3]
        pos += 3
    buf, sems = refs[pos], refs[pos + 1]
    for e in range(n):
        @pl.when(flags[e] > 0)
        def _():
            pltpu.make_async_copy(entries[e], buf.at[e], sems.at[e]).start()

    if first:
        m_ref[...] = jnp.full(m_ref.shape, -jnp.inf, F32)
        l_ref[...] = jnp.zeros(l_ref.shape, F32)
        acc_ref[...] = jnp.zeros(acc_ref.shape, F32)
    else:
        m_ref[...] = m_in[...]
        l_ref[...] = l_in[...]
        acc_ref[...] = acc_in[...]

    def visit(e, carry):
        @pl.when(flags[e] > 0)
        def _():
            pltpu.make_async_copy(entries[0], buf.at[e], sems.at[e]).wait()
            k = buf[e, :, :HEAD_SIZE]
            v = buf[e, :, HEAD_SIZE:]
            for h in range(2):
                for r in range(0, BT, ROWS):
                    q = q_ref[r : r + ROWS, h * HEAD_SIZE : (h + 1) * HEAD_SIZE]
                    s = dot_t(q, k) * C2
                    if diag:
                        row = lax.broadcasted_iota(jnp.int32, (ROWS, BT), 0) + r
                        col = lax.broadcasted_iota(jnp.int32, (ROWS, BT), 1)
                        s = jnp.where(col <= row + e * BT, s, -jnp.inf)
                    at = slice(h * BT + r, h * BT + r + ROWS)
                    m_old = m_ref[at, :]
                    m_new = jnp.maximum(m_old, jnp.max(s, axis=1, keepdims=True))
                    alpha = jnp.exp2(m_old - m_new)
                    p = jnp.exp2(s - m_new[:, :1])
                    m_ref[at, :] = m_new
                    l_ref[at, :] = l_ref[at, :] * alpha + jnp.sum(p, axis=1, keepdims=True)
                    acc_ref[at, :] = acc_ref[at, :] * alpha + jnp.dot(
                        p.astype(BF16), v, preferred_element_type=F32
                    )

        return carry

    lax.fori_loop(0, n, visit, 0)
    if last:
        for h in range(2):
            at = slice(h * BT, (h + 1) * BT)
            total = l_ref[at, :]
            attn_ref[:, h * HEAD_SIZE : (h + 1) * HEAD_SIZE] = (acc_ref[at, :] / total).astype(BF16)
            lse = m_ref[at, :] + jnp.log2(total)
            lse_ref[h : h + 1, :] = jnp.transpose(lse)[0:1, :]


def fwd_call(flags, q, state, entries, diag=False, last=False):
    n = len(entries)
    first = state is None
    vm = pl.BlockSpec(memory_space=pltpu.VMEM)
    state_shape = tuple(jax.ShapeDtypeStruct((2 * BT, HEAD_SIZE), F32) for _ in range(3))
    scratch = [pltpu.VMEM((n, BT, 2 * HEAD_SIZE), BF16), pltpu.SemaphoreType.DMA((n,))]
    if last:
        out_shape = (jax.ShapeDtypeStruct((BT, 2 * HEAD_SIZE), BF16), jax.ShapeDtypeStruct((2, BT), F32))
        scratch = [pltpu.VMEM((2 * BT, HEAD_SIZE), F32) for _ in range(3)] + scratch
    else:
        out_shape = state_shape
    return pl.pallas_call(
        functools.partial(fwd_body, n, diag, first, last),
        out_shape=out_shape,
        in_specs=[pl.BlockSpec(memory_space=pltpu.SMEM), vm]
        + ([] if first else [vm] * 3)
        + [pl.BlockSpec(memory_space=pl.ANY)] * n,
        out_specs=tuple(vm for _ in out_shape),
        scratch_shapes=scratch,
        name="fwd",
        cost_estimate=pl.CostEstimate(flops=n * 268435456, transcendentals=n * 524288, bytes_accessed=n * 262144),
    )(flags, q, *(() if first else state), *entries)


def bwd_body(n, diag, first, last, *refs):
    flags, q_ref, do_ref, attn_ref, lse_ref = refs[:5]
    pos = 5
    if not first:
        dq_in = refs[pos]
        pos += 1
    entries = refs[pos : pos + n]
    pos += n
    dq_out = refs[pos]
    pos += 1
    outs = refs[pos : pos + n]
    pos += n
    dq, delta_ref, buf, obuf, sems, osems = refs[pos : pos + 6]
    for e in range(n):
        @pl.when(flags[e] > 0)
        def _():
            pltpu.make_async_copy(entries[e], buf.at[e], sems.at[e]).start()

    dq[...] = jnp.zeros(dq.shape, F32) if first else dq_in[...]
    for h in range(2):
        cols = slice(h * HEAD_SIZE, (h + 1) * HEAD_SIZE)
        prod = do_ref[:, cols].astype(F32) * attn_ref[:, cols].astype(F32)
        delta_ref[h : h + 1, :] = jnp.sum(jnp.transpose(prod), axis=0, keepdims=True)

    def visit(e, carry):
        @pl.when(flags[e] > 0)
        def _():
            pltpu.make_async_copy(entries[0], buf.at[e], sems.at[e]).wait()
            for r in range(0, BT, ROWS):
                k = buf[e, r : r + ROWS, :HEAD_SIZE]
                v = buf[e, r : r + ROWS, HEAD_SIZE:]
                dk = jnp.zeros((ROWS, HEAD_SIZE), F32)
                dv = jnp.zeros((ROWS, HEAD_SIZE), F32)
                for h in range(2):
                    cols = slice(h * HEAD_SIZE, (h + 1) * HEAD_SIZE)
                    q = q_ref[:, cols]
                    do = do_ref[:, cols]
                    p = jnp.exp2(dot_t(k, q) * C2 - lse_ref[h : h + 1, :])
                    if diag:
                        row = lax.broadcasted_iota(jnp.int32, (ROWS, BT), 0) + r
                        col = lax.broadcasted_iota(jnp.int32, (ROWS, BT), 1)
                        p = jnp.where(row <= col + e * BT, p, 0.0)
                    ds = (p * (dot_t(v, do) - delta_ref[h : h + 1, :]) * SCALE).astype(BF16)
                    dv = dv + jnp.dot(p.astype(BF16), do, preferred_element_type=F32)
                    dk = dk + jnp.dot(ds, q, preferred_element_type=F32)
                    dq[h] = dq[h] + lax.dot_general(
                        k, ds, (((0,), (0,)), ((), ())), preferred_element_type=F32
                    )
                obuf[e, r : r + ROWS, :HEAD_SIZE] = dk.astype(BF16)
                obuf[e, r : r + ROWS, HEAD_SIZE:] = dv.astype(BF16)

        @pl.when(flags[e] <= 0)
        def _():
            obuf[e] = jnp.zeros((BT, 2 * HEAD_SIZE), BF16)

        return carry

    lax.fori_loop(0, n, visit, 0)
    for e in range(n):
        pltpu.make_async_copy(obuf.at[e], outs[e], osems.at[e]).start()
    if last:
        for h in range(2):
            dq_out[:, h * HEAD_SIZE : (h + 1) * HEAD_SIZE] = jnp.transpose(dq[h])
    else:
        dq_out[...] = dq[...]
    for e in range(n):
        pltpu.make_async_copy(obuf.at[e], outs[e], osems.at[e]).wait()


def bwd_call(flags, q, do, attn, lse, dq, entries, diag=False, last=False):
    n = len(entries)
    first = dq is None
    vm = pl.BlockSpec(memory_space=pltpu.VMEM)
    anyspace = pl.BlockSpec(memory_space=pl.ANY)
    dq_shape = (BT, 2 * HEAD_SIZE) if last else (2, HEAD_SIZE, BT)
    res = pl.pallas_call(
        functools.partial(bwd_body, n, diag, first, last),
        out_shape=(jax.ShapeDtypeStruct(dq_shape, F32),)
        + tuple(jax.ShapeDtypeStruct((BT, 2 * HEAD_SIZE), BF16) for _ in range(n)),
        in_specs=[pl.BlockSpec(memory_space=pltpu.SMEM)] + [vm] * (4 if first else 5) + [anyspace] * n,
        out_specs=(vm,) + (anyspace,) * n,
        scratch_shapes=[
            pltpu.VMEM((2, HEAD_SIZE, BT), F32),
            pltpu.VMEM((2, BT), F32),
            pltpu.VMEM((n, BT, 2 * HEAD_SIZE), BF16),
            pltpu.VMEM((n, BT, 2 * HEAD_SIZE), BF16),
            pltpu.SemaphoreType.DMA((n,)),
            pltpu.SemaphoreType.DMA((n,)),
        ],
        name="bwd",
        cost_estimate=pl.CostEstimate(flops=n * 671088640, transcendentals=n * 524288, bytes_accessed=n * 524288),
    )(flags, q, do, attn, lse, *(() if first else (dq,)), *entries)
    return res[0], res[1:]


def moves(rule):
    pairs = []
    for b in range(NB):
        to = rule(b // 8, b // 2 % 4, b % 2)
        if to is not None:
            x, y, c = to
            pairs.append((b, 8 * x + 2 * y + c))
    return pairs


def send(value, rule):
    return lax.ppermute(value, "ctx", moves(rule))


def swap(value):
    return send(value, lambda x, y, c: (x, y, 1 - c))


def added(*terms):
    total = terms[0].astype(F32)
    for t in terms[1:]:
        total = total + t.astype(F32)
    return total.astype(BF16)


def scatter_wout(terms, x, y, c):
    v = terms.reshape(4, 4, 2, 128, 256)
    keep = lax.dynamic_index_in_dim(v, c, 2, keepdims=False)
    give = lax.dynamic_index_in_dim(v, 1 - c, 2, keepdims=False)
    v = added(keep, swap(give))
    total = lax.dynamic_index_in_dim(v, y, 1, keepdims=False).astype(F32)
    for s in (1, 2, 3):
        part = lax.dynamic_index_in_dim(v, (y + s) % 4, 1, keepdims=False)
        total = total + send(part, lambda x, y, c: (x, (y + s) % 4, c)).astype(F32)
    low = total.astype(BF16)
    out = lax.dynamic_index_in_dim(total, x, 0, keepdims=False)
    for s in (1, 2, 3):
        part = lax.dynamic_index_in_dim(low, (x + s) % 4, 0, keepdims=False)
        out = out + send(part, lambda x, y, c: ((x + s) % 4, y, c)).astype(F32)
    return out


def per_device(query_proj, projected_keys, projected_values, w_out, attended_blocks, grad_out):
    rank = lax.axis_index("ctx")
    x, y, c = rank // 8, rank // 2 % 4, rank % 2
    listed = lax.dynamic_index_in_dim(attended_blocks, rank, 0, keepdims=False)

    piece = lax.all_gather(grad_out, "head", axis=1, tiled=True)

    own = jnp.concatenate([projected_keys, projected_values], 1)
    x1 = send(own, lambda x, y, c: (x + 1, y, c) if x < 3 else None)
    near1 = send(own, lambda x, y, c: (x, y + 1, c) if y < 3 else None)
    near2 = send(own, lambda x, y, c: (x, y + 2, c) if y < 2 else None)
    near3 = send(own, lambda x, y, c: (x, 3, c) if y == 0 else None)
    wrap1 = send(x1, lambda x, y, c: (x, 0, c) if y == 3 else None)
    wrap2 = send(x1, lambda x, y, c: (x, y - 2, c) if y >= 2 else None)
    wrap3 = send(x1, lambda x, y, c: (x, y - 1, c) if y >= 1 else None)
    d4 = x1
    d8 = send(x1, lambda x, y, c: (x + 1, y, c) if x < 3 else None)
    d1 = jnp.where(y == 0, wrap1, near1)
    d2 = jnp.where(y < 2, wrap2, near2)
    d3 = jnp.where(y == 3, near3, wrap3)
    d5 = send(d1, lambda x, y, c: (x + 1, y, c) if x < 3 else None)
    b6 = send(d2, lambda x, y, c: (x + 1, y, 0) if x < 3 and c == 1 else None)
    mine = {0: own, 1: d1, 2: d2, 3: d3, 4: d4, 5: d5, 8: d8}
    other = {d: swap(mine[d]) for d in range(6)}
    other[6] = b6

    def live(keys):
        shifts = jnp.stack([jnp.int32(2 * d) if kind == "a" else 2 * d - 1 + 2 * c for kind, d in keys])
        wanted = rank - shifts
        hit = (listed[None, :] == wanted[:, None]) & (wanted[:, None] >= 0) & (shifts[:, None] >= 0)
        return jnp.any(hit, 1).astype(jnp.int32)

    def blocks(keys):
        return [mine[d] if kind == "a" else other[d] for kind, d in keys]

    keys0 = [("a", 0), ("b", 0)]
    keys1 = [(kind, d) for d in (1, 2, 3, 4) for kind in ("a", "b")]
    keys2 = [("a", 5), ("b", 5), ("b", 6), ("a", 8)]
    live0, live1, live2 = live(keys0), live(keys1), live(keys2)
    state = fwd_call(live0, query_proj, None, blocks(keys0), diag=True)
    state = fwd_call(live1, query_proj, state, blocks(keys1))
    attn, lse = fwd_call(live2, query_proj, state, blocks(keys2), last=True)

    out_terms = jnp.dot(attn, w_out, preferred_element_type=F32).astype(BF16)
    layer_out = lax.psum_scatter(out_terms, "head", scatter_dimension=1, tiled=True)
    grad_attn = lax.dot_general(
        piece, w_out, (((1,), (1,)), ((), ())), preferred_element_type=F32
    ).astype(BF16)
    weight_terms = lax.dot_general(
        piece, attn, (((0,), (0,)), ((), ())), preferred_element_type=F32
    ).astype(BF16)

    dq, far = bwd_call(live2, query_proj, grad_attn, attn, lse, None, blocks(keys2))
    a5, g5, g6, a8 = far
    t5 = added(a5, swap(g5))
    back = lambda x, y, c: (x - 1, y, c) if x > 0 else None
    r5 = send(t5, back)
    r8 = send(a8, back)
    r6 = send(g6, lambda x, y, c: (x - 1, y, 1) if x > 0 and c == 0 else None)
    dq, close = bwd_call(live1, query_proj, grad_attn, attn, lse, dq, blocks(keys1))
    a1, g1, a2, g2, a3, g3, a4, g4 = close
    t1 = added(a1, swap(g1), r5)
    t2 = added(a2, swap(g2), r6)
    t3 = added(a3, swap(g3))
    s1 = send(t1, lambda x, y, c: (x, (y - 1) % 4, c))
    s2 = send(t2, lambda x, y, c: (x, (y - 2) % 4, c))
    s3 = send(t3, lambda x, y, c: (x, (y - 3) % 4, c))
    grad_query, (a0, g0) = bwd_call(live0, query_proj, grad_attn, attn, lse, dq, blocks(keys0), diag=True, last=True)
    zero = jnp.zeros((), F32)

    def kept(cond, v):
        return jnp.where(cond, v.astype(F32), zero)

    t4 = (
        a4.astype(F32) + swap(g4).astype(F32) + r8.astype(F32)
        + kept(y == 3, s1) + kept(y >= 2, s2) + kept(y >= 1, s3)
    ).astype(BF16)
    r4 = send(t4, back)
    total = (
        a0.astype(F32) + swap(g0).astype(F32) + r4.astype(F32)
        + kept(y < 3, s1) + kept(y < 2, s2) + kept(y < 1, s3)
    )
    grad_key = total[:, :HEAD_SIZE]
    grad_value = total[:, HEAD_SIZE:]
    grad_wout = scatter_wout(weight_terms, x, y, c).T
    return (layer_out, grad_query, grad_key, grad_value, grad_wout)


def solution(mesh):
    return jax.shard_map(
        per_device,
        mesh=mesh,
        in_specs=(
            P("ctx", "head"),
            P("ctx", "head"),
            P("ctx", "head"),
            P("head", None),
            P(),
            P("ctx", "head"),
        ),
        out_specs=(
            P("ctx", "head"),
            P("ctx", "head"),
            P("ctx", "head"),
            P("ctx", "head"),
            P("head", "ctx"),
        ),
        check_vma=False,
    )
```

```python
import functools

import jax
import jax.numpy as jnp
from jax import lax
from jax.experimental import pallas as pl
from jax.experimental.pallas import tpu as pltpu
from jax.sharding import PartitionSpec as P

HEAD_SIZE = 128
BT = 512
KV = 2 * BT
NB = 32
SCALE = HEAD_SIZE**-0.5
LOG2E = 1.4426950408889634
C2 = SCALE * LOG2E
ROWS = 256
F32 = jnp.float32
BF16 = jnp.bfloat16


VM = pl.BlockSpec(memory_space=pltpu.VMEM)
SM = pl.BlockSpec(memory_space=pltpu.SMEM)
ANY = pl.BlockSpec(memory_space=pl.ANY)


def dot_t(a, b):
    return lax.dot_general(a, b, (((1,), (1,)), ((), ())), preferred_element_type=F32)


def fetch(flags, base, sources, buf, sems):
    for e, (ref, row) in enumerate(sources):
        @pl.when(flags[2 * (base + e)] + flags[2 * (base + e) + 1] > 0)
        def _():
            pltpu.make_async_copy(ref.at[pl.ds(row, KV)], buf.at[e], sems.at[e]).start()


def walk(visit, n, diag):
    if diag:
        lax.fori_loop(0, 2, lambda i, carry: visit(True, i * diag, carry), 0)
        lax.fori_loop(0, n - 2, lambda i, carry: visit(False, jnp.where(i < diag - 1, i + 1, i + 2), carry), 0)
    else:
        lax.fori_loop(0, n, lambda i, carry: visit(False, i, carry), 0)


def fwd_body(base, plan, diag, first, last, *refs):
    n = len(plan)
    count = 1 + max(i for i, _ in plan)
    flags, q_ref = refs[0], refs[1]
    pos = 2
    if not first:
        m_in, l_in, acc_in = refs[pos : pos + 3]
        pos += 3
    arrays = refs[pos : pos + count]
    pos += count
    if last:
        own_ref, sib_ref, lse_ref = refs[pos : pos + 3]
        pos += 3
    m_ref, l_ref, acc_ref = refs[pos : pos + 3]
    buf, sems = refs[pos + 3 : pos + 5]
    fetch(flags, base, [(arrays[i], row) for i, row in plan], buf, sems)
    if first:
        m_ref[...] = jnp.full(m_ref.shape, -jnp.inf, F32)
        l_ref[...] = jnp.zeros(l_ref.shape, F32)
        acc_ref[...] = jnp.zeros(acc_ref.shape, F32)
    else:
        m_ref[...] = m_in[...]
        l_ref[...] = l_in[...]
        acc_ref[...] = acc_in[...]

    def unit(e, h, masked):
        k = buf[e, :BT, :]
        v = buf[e, BT:, :]
        for r in range(0, BT, ROWS):
            s = dot_t(q_ref[h, r : r + ROWS, :], k) * C2
            if masked:
                row = lax.broadcasted_iota(jnp.int32, (ROWS, BT), 0) + r
                col = lax.broadcasted_iota(jnp.int32, (ROWS, BT), 1)
                near = jnp.where((e == 0) & (h == 0) | (e == diag) & (h == 1), 0, BT)
                s = jnp.where(col <= row + near, s, -jnp.inf)
            at = slice(r, r + ROWS)
            m_old = m_ref[h, at, :]
            m_new = jnp.maximum(m_old, jnp.max(s, axis=1, keepdims=True))
            alpha = jnp.exp2(m_old - m_new)
            p = jnp.exp2(s - m_new[:, :1])
            m_ref[h, at, :] = m_new
            l_ref[h, at, :] = l_ref[h, at, :] * alpha + jnp.sum(p, axis=1, keepdims=True)
            acc_ref[h, at, :] = acc_ref[h, at, :] * alpha + jnp.dot(
                p.astype(BF16), v, preferred_element_type=F32
            )

    def visit(masked, e, carry):
        @pl.when(flags[2 * (base + e)] + flags[2 * (base + e) + 1] > 0)
        def _():
            pltpu.make_async_copy(arrays[0].at[pl.ds(0, KV)], buf.at[e], sems.at[e]).wait()

            def one(h, c2):
                @pl.when(flags[2 * (base + e) + h] > 0)
                def _():
                    unit(e, h, masked)

                return c2

            lax.fori_loop(0, 2, one, 0)

        return carry

    walk(visit, n, diag)
    if last:
        for h, ref in ((0, own_ref), (1, sib_ref)):
            total = l_ref[h]
            ref[...] = (acc_ref[h] / total).astype(BF16)
            lse_ref[h : h + 1, :] = jnp.transpose(m_ref[h] + jnp.log2(total))[0:1, :]


def fwd_call(flags, base, q2, state, arrays, plan, diag=0, last=False):
    n = len(plan)
    first = state is None
    state_shape = (2, BT, HEAD_SIZE)
    scratch = [pltpu.VMEM((n, KV, HEAD_SIZE), BF16), pltpu.SemaphoreType.DMA((n,))]
    if last:
        out_shape = (
            jax.ShapeDtypeStruct((BT, HEAD_SIZE), BF16),
            jax.ShapeDtypeStruct((BT, HEAD_SIZE), BF16),
            jax.ShapeDtypeStruct((2, BT), F32),
        )
        scratch = [pltpu.VMEM(state_shape, F32)] * 3 + scratch
    else:
        out_shape = (jax.ShapeDtypeStruct(state_shape, F32),) * 3
    return pl.pallas_call(
        functools.partial(fwd_body, base, plan, diag, first, last),
        out_shape=out_shape,
        in_specs=[SM, VM] + ([] if first else [VM] * 3) + [ANY] * len(arrays),
        out_specs=tuple(VM for _ in out_shape),
        scratch_shapes=scratch,
        name="fwd",
        cost_estimate=pl.CostEstimate(flops=n * 268435456, transcendentals=n * 524288, bytes_accessed=n * 262144),
    )(flags, q2, *(() if first else state), *arrays)


def bwd_body(base, plan, diag, first, last, *refs):
    n = len(plan)
    half = n // 2
    count = 1 + max(i for i, _ in plan)
    flags, q_ref, do_ref, own_ref, sib_ref, lse_ref = refs[:6]
    pos = 6
    if not first:
        dq_in = refs[pos]
        pos += 1
    arrays = refs[pos : pos + count]
    pos += count
    if last:
        dq_own, dq_sib = refs[pos : pos + 2]
        pos += 2
    else:
        dq_out = refs[pos]
        pos += 1
    keep_ref, give_ref = refs[pos : pos + 2]
    pos += 2
    dq, delta_ref, dkv, buf, obuf, sems, osems = refs[pos : pos + 7]
    fetch(flags, base, [(arrays[i], row) for i, row in plan], buf, sems)
    dq[...] = jnp.zeros(dq.shape, F32) if first else dq_in[...]
    for h, ref in ((0, own_ref), (1, sib_ref)):
        prod = do_ref[h].astype(F32) * ref[...].astype(F32)
        delta_ref[h : h + 1, :] = jnp.sum(jnp.transpose(prod), axis=0, keepdims=True)

    def unit(e, h, masked):
        q = q_ref[h]
        do = do_ref[h]
        lse = lse_ref[pl.ds(h, 1), :]
        delta = delta_ref[pl.ds(h, 1), :]
        for r in range(0, BT, ROWS):
            at = slice(r, r + ROWS)
            vt = slice(BT + r, BT + r + ROWS)
            k = buf[e, at, :]
            p = jnp.exp2(dot_t(k, q) * C2 - lse)
            if masked:
                row = lax.broadcasted_iota(jnp.int32, (ROWS, BT), 0) + r
                col = lax.broadcasted_iota(jnp.int32, (ROWS, BT), 1)
                near = jnp.where((e == 0) & (h == 0) | (e == diag) & (h == 1), 0, BT)
                p = jnp.where(row <= col + near, p, 0.0)
            ds = (p * (dot_t(buf[e, vt, :], do) - delta) * SCALE).astype(BF16)
            dkv[vt, :] += jnp.dot(p.astype(BF16), do, preferred_element_type=F32)
            dkv[at, :] += jnp.dot(ds, q, preferred_element_type=F32)
            dq[h] += lax.dot_general(k, ds, (((0,), (0,)), ((), ())), preferred_element_type=F32)

    def visit(masked, e, carry):
        on = flags[2 * (base + e)] + flags[2 * (base + e) + 1] > 0

        @pl.when(on)
        def _():
            pltpu.make_async_copy(arrays[0].at[pl.ds(0, KV)], buf.at[e], sems.at[e]).wait()
            dkv[...] = jnp.zeros(dkv.shape, F32)

            def one(h, c2):
                @pl.when(flags[2 * (base + e) + h] > 0)
                def _():
                    unit(e, h, masked)

                return c2

            lax.fori_loop(0, 2, one, 0)
            obuf[e] = dkv[...].astype(BF16)

        @pl.when(jnp.logical_not(on))
        def _():
            obuf[e] = jnp.zeros((KV, HEAD_SIZE), BF16)

        @pl.when(e < half)
        def _():
            pltpu.make_async_copy(obuf.at[e], keep_ref.at[pl.ds(e * KV, KV)], osems.at[e]).start()

        @pl.when(e >= half)
        def _():
            pltpu.make_async_copy(obuf.at[e], give_ref.at[pl.ds((e - half) * KV, KV)], osems.at[e]).start()

        return carry

    walk(visit, n, diag)
    if last:
        dq_own[...] = jnp.transpose(dq[0])
        dq_sib[...] = jnp.transpose(dq[1])
    else:
        dq_out[...] = dq[...]
    for e in range(n):
        pltpu.make_async_copy(obuf.at[e], keep_ref.at[pl.ds(0, KV)], osems.at[e]).wait()


def bwd_call(flags, base, q2, do2, own, sib, lse, dq, arrays, plan, diag=0, last=False):
    n = len(plan)
    first = dq is None
    dq_shape = (2, HEAD_SIZE, BT)
    head = jax.ShapeDtypeStruct((BT, HEAD_SIZE), F32)
    dq_outs = (head, head) if last else (jax.ShapeDtypeStruct(dq_shape, F32),)
    part = jax.ShapeDtypeStruct((n // 2 * KV, HEAD_SIZE), BF16)
    return pl.pallas_call(
        functools.partial(bwd_body, base, plan, diag, first, last),
        out_shape=dq_outs + (part, part),
        in_specs=[SM] + [VM] * (5 if first else 6) + [ANY] * len(arrays),
        out_specs=(VM,) * len(dq_outs) + (ANY, ANY),
        scratch_shapes=[
            pltpu.VMEM(dq_shape, F32),
            pltpu.VMEM((2, BT), F32),
            pltpu.VMEM((KV, HEAD_SIZE), F32),
            pltpu.VMEM((n, KV, HEAD_SIZE), BF16),
            pltpu.VMEM((n, KV, HEAD_SIZE), BF16),
            pltpu.SemaphoreType.DMA((n,)),
            pltpu.SemaphoreType.DMA((n,)),
        ],
        name="bwd",
        cost_estimate=pl.CostEstimate(flops=n * 671088640, transcendentals=n * 524288, bytes_accessed=n * 524288),
    )(flags, q2, do2, own, sib, lse, *(() if first else (dq,)), *arrays)


def grad_attn_body(g_ref, w_ref, out_ref, acc):
    @pl.when(pl.program_id(0) == 0)
    def _():
        acc[...] = jnp.zeros(acc.shape, F32)

    acc[...] += dot_t(g_ref[...], w_ref[...])

    @pl.when(pl.program_id(0) == pl.num_programs(0) - 1)
    def _():
        out_ref[...] = acc[...].astype(BF16)


def grad_attn_call(piece, w_out):
    rows, cols = piece.shape
    wide = 1024
    return pl.pallas_call(
        grad_attn_body,
        grid=(cols // wide,),
        out_shape=jax.ShapeDtypeStruct((rows, w_out.shape[0]), BF16),
        in_specs=[
            pl.BlockSpec((rows, wide), lambda i: (0, i)),
            pl.BlockSpec((w_out.shape[0], wide), lambda i: (0, i)),
        ],
        out_specs=pl.BlockSpec((rows, w_out.shape[0]), lambda i: (0, 0)),
        scratch_shapes=[pltpu.VMEM((rows, w_out.shape[0]), F32)],
        name="grad_attn",
        cost_estimate=pl.CostEstimate(flops=1073741824, transcendentals=0, bytes_accessed=6815744),
    )(piece, w_out)


ORDER = (0, 2, 1, 3)


def order(i):
    return (i % 2) * 2 + i // 2


def wout_body(where_ref, a_ref, *refs):
    keep_ref, give_ref, at = refs[4:]

    @pl.when(pl.program_id(0) == 0)
    def _():
        at[...] = jnp.transpose(a_ref[...])

    for i in range(4):
        term = jnp.dot(at[...], refs[i][...], preferred_element_type=F32).astype(BF16)

        @pl.when(where_ref[2] == 0)
        def _():
            keep_ref[i] = term[:, :128]
            give_ref[i] = term[:, 128:]

        @pl.when(where_ref[2] == 1)
        def _():
            keep_ref[i] = term[:, 128:]
            give_ref[i] = term[:, :128]


def wout_call(where, attn, piece):
    rows, width = attn.shape

    def column(i):
        return lambda p, w: (0, 4 * (w[0] ^ ORDER[i]) + (w[1] ^ order(p)))

    out = jax.ShapeDtypeStruct((16, width, 128), BF16)
    spec = pl.BlockSpec((4, width, 128), lambda p, w: (p, 0, 0))
    return pl.pallas_call(
        wout_body,
        grid_spec=pltpu.PrefetchScalarGridSpec(
            num_scalar_prefetch=1,
            grid=(4,),
            in_specs=[pl.BlockSpec((rows, width), lambda p, w: (0, 0))]
            + [pl.BlockSpec((rows, 256), column(i)) for i in range(4)],
            out_specs=[spec, spec],
            scratch_shapes=[pltpu.VMEM((width, rows), BF16)],
        ),
        out_shape=(out, out),
        name="wout_terms",
        cost_estimate=pl.CostEstimate(flops=1073741824, transcendentals=0, bytes_accessed=6553600),
    )(where, attn, *([piece] * 4))


def send(value, rule):
    pairs = []
    for b in range(NB):
        to = rule(b // 8, b // 2 % 4, b % 2)
        if to is not None:
            x, y, c = to
            pairs.append((b, 8 * x + 2 * y + c))
    return lax.ppermute(value, "ctx", pairs)


def swap(value):
    return send(value, lambda x, y, c: (x, y, 1 - c))


def ahead(value):
    return send(value, lambda x, y, c: (x + 1, y, c) if x < 3 else None)


def back(value):
    return send(value, lambda x, y, c: (x - 1, y, c) if x > 0 else None)


def along(value, k):
    return send(value, lambda x, y, c: (x, (y + k) % 4, c))


def bf(v):
    return v.astype(BF16)


def f32(v):
    return v.astype(F32)


def per_device(query_proj, projected_keys, projected_values, w_out, attended_blocks, grad_out):
    rank = lax.axis_index("ctx")
    x, y, c = rank // 8, rank // 2 % 4, rank % 2
    sib = rank + 1 - 2 * c

    piece = lax.all_gather(grad_out, "head", axis=1, tiled=True)

    def mine_of(v):
        return jnp.where(c == 0, v[:, :HEAD_SIZE], v[:, HEAD_SIZE:])

    def other_of(v):
        return jnp.where(c == 0, v[:, HEAD_SIZE:], v[:, :HEAD_SIZE])

    def joined(own, other):
        return jnp.where(c == 0, jnp.concatenate([own, other], 1), jnp.concatenate([other, own], 1))

    own = jnp.concatenate([projected_keys, projected_values], 0)
    x1 = ahead(own)
    ownx = swap(jnp.concatenate([projected_keys, projected_values, other_of(query_proj)], 0))
    d1 = along(jnp.where(y < 3, own, x1), 1)
    d2 = along(jnp.where(y < 2, own, x1), 2)
    d3 = along(jnp.where(y < 1, own, x1), 3)
    pre = jnp.concatenate([d1, d2, x1], 0)
    far = ahead(pre)
    prex = swap(pre)
    d3x = swap(d3)
    farx = swap(far)
    q2 = jnp.stack([mine_of(query_proj), ownx[KV:]])

    edge_d, mid_d, far_d = [0, 3], [1, 2, 4], [5, 6, 8]
    groups = ([0], [3, 1, 2, 4], edge_d, mid_d, far_d)
    keys = jnp.concatenate([b - 2 * jnp.array(d) for d in groups for b in (rank, sib)])
    lists = jnp.stack(
        [lax.dynamic_index_in_dim(attended_blocks, r, 0, keepdims=False) for r in (rank, sib)]
    )
    hit = jnp.any(lists[None] == keys[:, None, None], -1) & (keys >= 0)[:, None]
    flags = hit.astype(jnp.int32).reshape(-1)
    edge = ([own, d3, ownx, d3x], ((0, 0), (1, 0), (2, 0), (3, 0)))
    three = tuple((i, j * KV) for i in (0, 1) for j in (0, 1, 2))
    mid, outer = ([pre, prex], three), ([far, farx], three)
    near = ([d3, pre, d3x, prex], tuple((i + j, row) for i in (0, 2) for j, row in ((0, 0), (1, 0), (1, KV), (1, 2 * KV))))
    state = fwd_call(flags, 0, q2, None, [own, ownx], ((0, 0), (1, 0)), diag=1)
    state = fwd_call(flags, 2, q2, state, *near)
    attn_own, attn_sib, lse = fwd_call(flags, 20, q2, state, *outer, last=True)
    attn_other = swap(attn_sib)
    attn = joined(attn_own, attn_other)

    out_terms = bf(jnp.dot(attn, w_out, preferred_element_type=F32))
    layer_out = lax.psum_scatter(out_terms, "head", scatter_dimension=1, tiled=True)
    grad_attn = grad_attn_call(piece, w_out)
    do_sib = swap(other_of(grad_attn))
    do2 = jnp.stack([mine_of(grad_attn), do_sib])
    wkeep, wgive = wout_call(jnp.stack([x, y, c]), attn, piece)
    wcame = swap(wgive)

    def summed(n, parts, sent):
        low, high = [p[:n] for p in parts], [p[n : 2 * n] for p in parts]
        if sent is not None:
            low, high = low + [sent[:n]], high + [sent[n : 2 * n]]
        return low, bf(sum(f32(p) for p in high))

    args = (q2, do2, attn_own, attn_sib, lse)
    dq, keep, give = bwd_call(flags, 20, *args, None, *outer)
    got = swap(give)
    came = back(bf(f32(keep) + f32(got)))
    parts, gave = summed(8, [wkeep], wcame)
    wcame = send(gave, lambda x, y, c: (x, y ^ 1, c))
    dq, keep_e, give_e = bwd_call(flags, 10, *args, dq, *edge, diag=2)
    got_e = swap(give_e)
    s3 = along(bf(f32(keep_e[KV:]) + f32(got_e[KV:])), -3)
    dq_own, dq_sib, keep, give = bwd_call(flags, 14, *args, dq, *mid, last=True)
    got = swap(give)
    dq_other = swap(dq_sib)
    parts, gave = summed(4, parts, wcame)
    wcame = send(gave, lambda x, y, c: (x, y ^ 2, c))
    t1, t2, t4 = [f32(keep[at]) + f32(got[at]) + f32(came[at]) for at in (slice(i, i + KV) for i in (0, KV, 2 * KV))]
    s1 = along(bf(t1), -1)
    s2 = along(bf(t2), -2)
    parts, gave = summed(2, parts, wcame)
    wcame = send(gave, lambda x, y, c: (x ^ 1, y, c))

    def kept(cond, v):
        return jnp.where(cond, f32(v), 0.0)

    t4 = t4 + kept(y == 3, s1) + kept(y >= 2, s2) + kept(y >= 1, s3)
    r4 = back(bf(t4))
    parts, gave = summed(1, parts, wcame)
    wcame = send(gave, lambda x, y, c: (x ^ 2, y, c))
    grad_wout = sum(f32(p[0]) for p in parts) + f32(wcame[0])
    grad_query = joined(dq_own, dq_other)
    total = f32(keep_e[:KV]) + f32(got_e[:KV]) + kept(y < 3, s1) + kept(y < 2, s2) + kept(y < 1, s3) + f32(r4)
    return (layer_out, grad_query, total[:BT], total[BT:], grad_wout)


def solution(mesh):
    return jax.shard_map(
        per_device,
        mesh=mesh,
        in_specs=(
            P("ctx", "head"),
            P("ctx", "head"),
            P("ctx", "head"),
            P("head", None),
            P(),
            P("ctx", "head"),
        ),
        out_specs=(
            P("ctx", "head"),
            P("ctx", "head"),
            P("ctx", "head"),
            P("ctx", "head"),
            P("head", "ctx"),
        ),
        check_vma=False,
    )
```

```python
import functools

import jax
import jax.numpy as jnp
from jax import lax
from jax.experimental import pallas as pl
from jax.experimental.pallas import tpu as pltpu
from jax.sharding import PartitionSpec as P

HEAD_SIZE = 128
BT = 512
KV = 2 * BT
NB = 32
SCALE = HEAD_SIZE**-0.5
LOG2E = 1.4426950408889634
C2 = SCALE * LOG2E
ROWS = 256
COLS = 512
F32 = jnp.float32
BF16 = jnp.bfloat16


VM = pl.BlockSpec(memory_space=pltpu.VMEM)
SM = pl.BlockSpec(memory_space=pltpu.SMEM)
ANY = pl.BlockSpec(memory_space=pl.ANY)


def dot_t(a, b):
    return lax.dot_general(a, b, (((1,), (1,)), ((), ())), preferred_element_type=F32)


def fetch(flags, base, sources, buf, sems):
    for e, (ref, row) in enumerate(sources):
        @pl.when(flags[2 * (base + e)] + flags[2 * (base + e) + 1] > 0)
        def _():
            pltpu.make_async_copy(ref.at[pl.ds(row, KV)], buf.at[e], sems.at[e]).start()


def walk(visit, n, diag):
    if diag:
        lax.fori_loop(0, 2, lambda i, carry: visit(True, i * diag, carry), 0)
        lax.fori_loop(0, n - 2, lambda i, carry: visit(False, jnp.where(i < diag - 1, i + 1, i + 2), carry), 0)
    else:
        lax.fori_loop(0, n, lambda i, carry: visit(False, i, carry), 0)


def fwd_body(base, plan, diag, first, last, *refs):
    n = len(plan)
    count = 1 + max(i for i, _ in plan)
    flags, q_ref = refs[0], refs[1]
    pos = 2
    if not first:
        ml_in, acc_in = refs[pos : pos + 2]
        pos += 2
    arrays = refs[pos : pos + count]
    pos += count
    if last:
        own_ref, sib_ref, lse_ref = refs[pos : pos + 3]
        pos += 3
    ml_ref, acc_ref, buf, sems = refs[pos : pos + 4]
    fetch(flags, base, [(arrays[i], row) for i, row in plan], buf, sems)
    if first:
        ml_ref[0] = jnp.full((2, BT), -jnp.inf, F32)
        ml_ref[1] = jnp.zeros((2, BT), F32)
        acc_ref[...] = jnp.zeros(acc_ref.shape, F32)
    else:
        ml_ref[...] = ml_in[...]
        acc_ref[...] = acc_in[...]

    def unit(e, h, masked):
        k = buf[e, :BT, :]
        v = buf[e, BT:, :]
        for r in range(0, BT, COLS):
            at = slice(r, r + COLS)
            s = dot_t(k, q_ref[h, at, :]) * C2
            if masked:
                row = lax.broadcasted_iota(jnp.int32, (BT, COLS), 0)
                col = lax.broadcasted_iota(jnp.int32, (BT, COLS), 1) + r
                near = jnp.where((e == 0) & (h == 0) | (e == diag) & (h == 1), 0, BT)
                s = jnp.where(row <= col + near, s, -jnp.inf)
            m_old = ml_ref[0, pl.ds(h, 1), at]
            m_new = jnp.maximum(m_old, jnp.max(s, axis=0, keepdims=True))
            alpha = jnp.exp2(m_old - m_new)
            p = jnp.exp2(s - m_new)
            ml_ref[0, pl.ds(h, 1), at] = m_new
            ml_ref[1, pl.ds(h, 1), at] = ml_ref[1, pl.ds(h, 1), at] * alpha + jnp.sum(p, axis=0, keepdims=True)
            acc_ref[h, :, at] = acc_ref[h, :, at] * alpha + lax.dot_general(
                v, p.astype(BF16), (((0,), (0,)), ((), ())), preferred_element_type=F32
            )

    def visit(masked, e, carry):
        @pl.when(flags[2 * (base + e)] + flags[2 * (base + e) + 1] > 0)
        def _():
            pltpu.make_async_copy(arrays[0].at[pl.ds(0, KV)], buf.at[e], sems.at[e]).wait()

            def one(h, c2):
                @pl.when(flags[2 * (base + e) + h] > 0)
                def _():
                    unit(e, h, masked)

                return c2

            lax.fori_loop(0, 2, one, 0)

        return carry

    walk(visit, n, diag)
    if last:
        lse_ref[...] = ml_ref[0] + jnp.log2(ml_ref[1])
        for h, ref in ((0, own_ref), (1, sib_ref)):
            ref[...] = jnp.transpose(acc_ref[h] / ml_ref[1, h : h + 1, :]).astype(BF16)


def fwd_call(flags, base, q2, state, arrays, plan, diag=0, last=False):
    n = len(plan)
    first = state is None
    shapes = ((2, 2, BT), (2, HEAD_SIZE, BT))
    scratch = [pltpu.VMEM((n, KV, HEAD_SIZE), BF16), pltpu.SemaphoreType.DMA((n,))]
    if last:
        out_shape = (
            jax.ShapeDtypeStruct((BT, HEAD_SIZE), BF16),
            jax.ShapeDtypeStruct((BT, HEAD_SIZE), BF16),
            jax.ShapeDtypeStruct((2, BT), F32),
        )
        scratch = [pltpu.VMEM(shape, F32) for shape in shapes] + scratch
    else:
        out_shape = tuple(jax.ShapeDtypeStruct(shape, F32) for shape in shapes)
    return pl.pallas_call(
        functools.partial(fwd_body, base, plan, diag, first, last),
        out_shape=out_shape,
        in_specs=[SM, VM] + ([] if first else [VM] * 2) + [ANY] * len(arrays),
        out_specs=tuple(VM for _ in out_shape),
        scratch_shapes=scratch,
        name="fwd",
        cost_estimate=pl.CostEstimate(flops=n * 268435456, transcendentals=n * 524288, bytes_accessed=n * 262144),
    )(flags, q2, *(() if first else state), *arrays)


def bwd_body(base, plan, diag, first, last, *refs):
    n = len(plan)
    half = n // 2
    count = 1 + max(i for i, _ in plan)
    flags, q_ref, do_own, do_sib, lse_ref = refs[:5]
    if first:
        own_ref, sib_ref = refs[5:7]
    else:
        dq_in, delta_in = refs[5:7]
    pos = 7
    arrays = refs[pos : pos + count]
    pos += count
    if last:
        dq_own, dq_sib = refs[pos : pos + 2]
        pos += 2
    else:
        dq_out, delta_out = refs[pos : pos + 2]
        pos += 2
    keep_ref, give_ref = refs[pos : pos + 2]
    pos += 2
    dq, delta_ref, do_ref, dkv, buf, obuf, sems, osems = refs[pos : pos + 8]
    fetch(flags, base, [(arrays[i], row) for i, row in plan], buf, sems)
    do_ref[0] = do_own[...]
    do_ref[1] = do_sib[...]
    if first:
        dq[...] = jnp.zeros(dq.shape, F32)
        for h, ref in ((0, own_ref), (1, sib_ref)):
            prod = do_ref[h].astype(F32) * ref[...].astype(F32)
            delta_ref[h : h + 1, :] = jnp.sum(jnp.transpose(prod), axis=0, keepdims=True)
    else:
        dq[...] = dq_in[...]
        delta_ref[...] = delta_in[...]

    def unit(e, h, masked):
        q = q_ref[h]
        do = do_ref[h]
        lse = lse_ref[pl.ds(h, 1), :]
        delta = delta_ref[pl.ds(h, 1), :]
        for r in range(0, BT, ROWS):
            at = slice(r, r + ROWS)
            vt = slice(BT + r, BT + r + ROWS)
            k = buf[e, at, :]
            p = jnp.exp2(dot_t(k, q) * C2 - lse)
            if masked:
                row = lax.broadcasted_iota(jnp.int32, (ROWS, BT), 0) + r
                col = lax.broadcasted_iota(jnp.int32, (ROWS, BT), 1)
                near = jnp.where((e == 0) & (h == 0) | (e == diag) & (h == 1), 0, BT)
                p = jnp.where(row <= col + near, p, 0.0)
            ds = (p * (dot_t(buf[e, vt, :], do) - delta) * SCALE).astype(BF16)
            dkv[vt, :] += jnp.dot(p.astype(BF16), do, preferred_element_type=F32)
            dkv[at, :] += jnp.dot(ds, q, preferred_element_type=F32)
            dq[h] += lax.dot_general(k, ds, (((0,), (0,)), ((), ())), preferred_element_type=F32)

    def visit(masked, e, carry):
        on = flags[2 * (base + e)] + flags[2 * (base + e) + 1] > 0

        @pl.when(on)
        def _():
            pltpu.make_async_copy(arrays[0].at[pl.ds(0, KV)], buf.at[e], sems.at[e]).wait()
            dkv[...] = jnp.zeros(dkv.shape, F32)

            def one(h, c2):
                @pl.when(flags[2 * (base + e) + h] > 0)
                def _():
                    unit(e, h, masked)

                return c2

            lax.fori_loop(0, 2, one, 0)
            obuf[e] = dkv[...].astype(BF16)

        @pl.when(jnp.logical_not(on))
        def _():
            obuf[e] = jnp.zeros((KV, HEAD_SIZE), BF16)

        @pl.when(e < half)
        def _():
            pltpu.make_async_copy(obuf.at[e], keep_ref.at[pl.ds(e * KV, KV)], osems.at[e]).start()

        @pl.when(e >= half)
        def _():
            pltpu.make_async_copy(obuf.at[e], give_ref.at[pl.ds((e - half) * KV, KV)], osems.at[e]).start()

        return carry

    walk(visit, n, diag)
    if last:
        dq_own[...] = jnp.transpose(dq[0])
        dq_sib[...] = jnp.transpose(dq[1])
    else:
        dq_out[...] = dq[...]
        delta_out[...] = delta_ref[...]
    for e in range(n):
        pltpu.make_async_copy(obuf.at[e], keep_ref.at[pl.ds(0, KV)], osems.at[e]).wait()


def bwd_call(flags, base, q2, do_own, do_sib, lse, state, arrays, plan, diag=0, first=False, last=False):
    n = len(plan)
    dq_shape = (2, HEAD_SIZE, BT)
    head = jax.ShapeDtypeStruct((BT, HEAD_SIZE), F32)
    dq_outs = (head, head) if last else (jax.ShapeDtypeStruct(dq_shape, F32), jax.ShapeDtypeStruct((2, BT), F32))
    part = jax.ShapeDtypeStruct((n // 2 * KV, HEAD_SIZE), BF16)
    return pl.pallas_call(
        functools.partial(bwd_body, base, plan, diag, first, last),
        out_shape=dq_outs + (part, part),
        in_specs=[SM] + [VM] * 6 + [ANY] * len(arrays),
        out_specs=(VM,) * len(dq_outs) + (ANY, ANY),
        scratch_shapes=[
            pltpu.VMEM(dq_shape, F32),
            pltpu.VMEM((2, BT), F32),
            pltpu.VMEM((2, BT, HEAD_SIZE), BF16),
            pltpu.VMEM((KV, HEAD_SIZE), F32),
            pltpu.VMEM((n, KV, HEAD_SIZE), BF16),
            pltpu.VMEM((n, KV, HEAD_SIZE), BF16),
            pltpu.SemaphoreType.DMA((n,)),
            pltpu.SemaphoreType.DMA((n,)),
        ],
        name="bwd",
        cost_estimate=pl.CostEstimate(flops=n * 671088640, transcendentals=n * 524288, bytes_accessed=n * 524288),
    )(flags, q2, do_own, do_sib, lse, *state, *arrays)


ORDER = (0, 2, 1, 3)


def order(i):
    return (i % 2) * 2 + i // 2


def grads_body(where_ref, a_ref, *refs):
    pieces, weights = refs[:4], refs[4:8]
    keep_ref, give_ref, mine_ref, other_ref, at, acc = refs[8:]
    step = pl.program_id(0)

    @pl.when(step == 0)
    def _():
        at[...] = jnp.transpose(a_ref[...])
        acc[...] = jnp.zeros(acc.shape, F32)

    first = where_ref[2] == 0
    total = acc[...]
    for i in range(4):
        piece = pieces[i][...]
        total = total + dot_t(piece, weights[i][...])
        term = jnp.dot(at[...], piece, preferred_element_type=F32).astype(BF16)
        keep_ref[i] = jnp.where(first, term[:, :128], term[:, 128:])
        give_ref[i] = jnp.where(first, term[:, 128:], term[:, :128])
    acc[...] = total

    @pl.when(step == pl.num_programs(0) - 1)
    def _():
        low = total.astype(BF16)
        mine_ref[...] = jnp.where(first, low[:, :128], low[:, 128:])
        other_ref[...] = jnp.where(first, low[:, 128:], low[:, :128])


def grads_call(where, attn, piece, w_out):
    rows, width = attn.shape

    def column(i):
        return lambda p, w: (0, 4 * (w[0] ^ ORDER[i]) + (w[1] ^ order(p)))

    out = jax.ShapeDtypeStruct((16, width, 128), BF16)
    spec = pl.BlockSpec((4, width, 128), lambda p, w: (p, 0, 0))
    return pl.pallas_call(
        grads_body,
        grid_spec=pltpu.PrefetchScalarGridSpec(
            num_scalar_prefetch=1,
            grid=(4,),
            in_specs=[pl.BlockSpec((rows, width), lambda p, w: (0, 0))]
            + [pl.BlockSpec((rows, 256), column(i)) for i in range(4)]
            + [pl.BlockSpec((width, 256), column(i)) for i in range(4)],
            out_specs=[spec, spec] + [pl.BlockSpec((rows, HEAD_SIZE), lambda p, w: (0, 0))] * 2,
            scratch_shapes=[pltpu.VMEM((width, rows), BF16), pltpu.VMEM((rows, width), F32)],
        ),
        out_shape=(out, out) + (jax.ShapeDtypeStruct((rows, HEAD_SIZE), BF16),) * 2,
        name="grads",
        cost_estimate=pl.CostEstimate(flops=2147483648, transcendentals=0, bytes_accessed=8912896),
    )(where, attn, *([piece] * 4), *([w_out] * 4))


def send(value, rule):
    pairs = []
    for b in range(NB):
        to = rule(b // 8, b // 2 % 4, b % 2)
        if to is not None:
            x, y, c = to
            pairs.append((b, 8 * x + 2 * y + c))
    return lax.ppermute(value, "ctx", pairs)


def swap(value):
    return send(value, lambda x, y, c: (x, y, 1 - c))


def ahead(value):
    return send(value, lambda x, y, c: (x + 1, y, c) if x < 3 else None)


def back(value):
    return send(value, lambda x, y, c: (x - 1, y, c) if x > 0 else None)


def along(value, k):
    return send(value, lambda x, y, c: (x, (y + k) % 4, c))


def bf(v):
    return v.astype(BF16)


def f32(v):
    return v.astype(F32)


def per_device(query_proj, projected_keys, projected_values, w_out, attended_blocks, grad_out):
    rank = lax.axis_index("ctx")
    x, y, c = rank // 8, rank // 2 % 4, rank % 2
    sib = rank + 1 - 2 * c

    piece = lax.all_gather(grad_out, "head", axis=1, tiled=True)

    def mine_of(v):
        return jnp.where(c == 0, v[:, :HEAD_SIZE], v[:, HEAD_SIZE:])

    def other_of(v):
        return jnp.where(c == 0, v[:, HEAD_SIZE:], v[:, :HEAD_SIZE])

    def joined(own, other):
        return jnp.where(c == 0, jnp.concatenate([own, other], 1), jnp.concatenate([other, own], 1))

    own = jnp.concatenate([projected_keys, projected_values], 0)
    x1 = ahead(own)
    ownx = swap(jnp.concatenate([projected_keys, projected_values, other_of(query_proj)], 0))
    d1 = along(jnp.where(y < 3, own, x1), 1)
    d2 = along(jnp.where(y < 2, own, x1), 2)
    d3 = along(jnp.where(y < 1, own, x1), 3)
    d8 = ahead(x1)
    x1x = swap(x1)
    pre = jnp.concatenate([d1, d2], 0)
    far = ahead(pre)
    prex = swap(pre)
    d3x = swap(d3)
    d8x = swap(d8)
    farx = swap(far)
    q2 = jnp.stack([mine_of(query_proj), ownx[KV:]])

    keys = jnp.concatenate([b - 2 * jnp.array(d) for d in ([0], [1, 2, 4, 3], [5, 6, 8]) for b in (rank, sib)])
    lists = jnp.stack(
        [lax.dynamic_index_in_dim(attended_blocks, r, 0, keepdims=False) for r in (rank, sib)]
    )
    hit = jnp.any(lists[None] == keys[:, None, None], -1) & (keys >= 0)[:, None]
    flags = hit.astype(jnp.int32).reshape(-1)
    self_blocks = ([own, ownx], ((0, 0), (1, 0)))
    near_blocks = ([pre, x1, d3, prex, x1x, d3x], ((0, 0), (0, KV), (1, 0), (2, 0), (3, 0), (3, KV), (4, 0), (5, 0)))
    far_blocks = ([far, d8, farx, d8x], ((0, 0), (0, KV), (1, 0), (2, 0), (2, KV), (3, 0)))
    state = fwd_call(flags, 0, q2, None, *self_blocks, diag=1)
    state = fwd_call(flags, 2, q2, state, *near_blocks)
    attn_own, attn_sib, lse = fwd_call(flags, 10, q2, state, *far_blocks, last=True)
    attn_other = swap(attn_sib)
    attn = joined(attn_own, attn_other)

    out_terms = bf(jnp.dot(attn, w_out, preferred_element_type=F32))
    layer_out = lax.psum_scatter(out_terms, "head", scatter_dimension=1, tiled=True)
    wkeep, wgive, do_own, do_other = grads_call(jnp.stack([x, y, c]), attn, piece, w_out)
    do_sib = swap(do_other)
    wcame = swap(wgive)

    def summed(n, parts, sent):
        low, high = [p[:n] for p in parts] + [sent[:n]], [p[n : 2 * n] for p in parts] + [sent[n : 2 * n]]
        return low, bf(sum(f32(p) for p in high))

    args = (q2, do_own, do_sib, lse)
    dq, delta, keep, give = bwd_call(flags, 10, *args, (attn_own, attn_sib), *far_blocks, first=True)
    got = swap(give)
    came = back(bf(f32(keep) + f32(got)))
    parts, gave = summed(8, [wkeep], wcame)
    wcame = send(gave, lambda x, y, c: (x, y ^ 1, c))
    dq, delta, keep, give = bwd_call(flags, 2, *args, (dq, delta), *near_blocks)
    got = swap(give)
    dq_own, dq_sib, keep0, give0 = bwd_call(flags, 0, *args, (dq, delta), *self_blocks, diag=1, last=True)
    got0 = swap(give0)
    dq_other = swap(dq_sib)
    parts, gave = summed(4, parts, wcame)
    wcame = send(gave, lambda x, y, c: (x, y ^ 2, c))
    t1, t2, t4 = [f32(keep[at]) + f32(got[at]) + f32(came[at]) for at in (slice(i, i + KV) for i in (0, KV, 2 * KV))]
    t3 = f32(keep[3 * KV :]) + f32(got[3 * KV :])
    s1 = along(bf(t1), -1)
    s2 = along(bf(t2), -2)
    s3 = along(bf(t3), -3)
    parts, gave = summed(2, parts, wcame)
    wcame = send(gave, lambda x, y, c: (x ^ 1, y, c))

    def kept(cond, v):
        return jnp.where(cond, f32(v), 0.0)

    r4 = back(bf(t4 + kept(y == 3, s1) + kept(y >= 2, s2) + kept(y >= 1, s3)))
    parts, gave = summed(1, parts, wcame)
    wcame = send(gave, lambda x, y, c: (x ^ 2, y, c))
    grad_wout = sum(f32(p[0]) for p in parts) + f32(wcame[0])
    grad_query = joined(dq_own, dq_other)
    total = f32(keep0) + f32(got0) + kept(y < 3, s1) + kept(y < 2, s2) + kept(y < 1, s3)
    total = lax.optimization_barrier(total)
    grad_key, grad_value = [total[at] + f32(r4[at]) for at in (slice(0, BT), slice(BT, KV))]
    return (layer_out, grad_query, grad_key, grad_value, grad_wout)


def solution(mesh):
    return jax.shard_map(
        per_device,
        mesh=mesh,
        in_specs=(
            P("ctx", "head"),
            P("ctx", "head"),
            P("ctx", "head"),
            P("head", None),
            P(),
            P("ctx", "head"),
        ),
        out_specs=(
            P("ctx", "head"),
            P("ctx", "head"),
            P("ctx", "head"),
            P("ctx", "head"),
            P("head", "ctx"),
        ),
        check_vma=False,
    )
```

```python
import functools

import jax
import jax.numpy as jnp
from jax import lax
from jax.experimental import pallas as pl
from jax.experimental.pallas import tpu as pltpu
from jax.sharding import PartitionSpec as P

HEAD_SIZE = 128
BT = 512
KV = 2 * BT
NB = 32
SCALE = HEAD_SIZE**-0.5
LOG2E = 1.4426950408889634
C2 = SCALE * LOG2E
ROWS = 256
COLS = 512
F32 = jnp.float32
BF16 = jnp.bfloat16


VM = pl.BlockSpec(memory_space=pltpu.VMEM)
SM = pl.BlockSpec(memory_space=pltpu.SMEM)
ANY = pl.BlockSpec(memory_space=pl.ANY)


def dot_t(a, b):
    return lax.dot_general(a, b, (((1,), (1,)), ((), ())), preferred_element_type=F32)


def fetch(flags, base, sources, buf, sems):
    for e, (ref, row) in enumerate(sources):
        @pl.when(flags[2 * (base + e)] + flags[2 * (base + e) + 1] > 0)
        def _():
            pltpu.make_async_copy(ref.at[pl.ds(row, KV)], buf.at[e], sems.at[e]).start()


def walk(visit, n, diag):
    if diag:
        lax.fori_loop(0, 2, lambda i, carry: visit(True, i * diag, carry), 0)
        lax.fori_loop(0, n - 2, lambda i, carry: visit(False, jnp.where(i < diag - 1, i + 1, i + 2), carry), 0)
    else:
        lax.fori_loop(0, n, lambda i, carry: visit(False, i, carry), 0)


def fwd_body(base, plan, diag, first, last, *refs):
    n = len(plan)
    count = 1 + max(i for i, _ in plan)
    flags, q_ref = refs[0], refs[1]
    pos = 2
    if not first:
        ml_in, acc_in = refs[pos : pos + 2]
        pos += 2
    arrays = refs[pos : pos + count]
    pos += count
    if last:
        own_ref, sib_ref, lse_ref = refs[pos : pos + 3]
        pos += 3
    ml_ref, acc_ref, buf, sems = refs[pos : pos + 4]
    fetch(flags, base, [(arrays[i], row) for i, row in plan], buf, sems)
    if first:
        ml_ref[0] = jnp.full((2, BT), -jnp.inf, F32)
        ml_ref[1] = jnp.zeros((2, BT), F32)
        acc_ref[...] = jnp.zeros(acc_ref.shape, F32)
    else:
        ml_ref[...] = ml_in[...]
        acc_ref[...] = acc_in[...]

    def unit(e, h, masked):
        k = buf[e, :BT, :]
        v = buf[e, BT:, :]
        for r in range(0, BT, COLS):
            at = slice(r, r + COLS)
            s = dot_t(k, q_ref[h, at, :]) * C2
            if masked:
                row = lax.broadcasted_iota(jnp.int32, (BT, COLS), 0)
                col = lax.broadcasted_iota(jnp.int32, (BT, COLS), 1) + r
                near = jnp.where((e == 0) & (h == 0) | (e == diag) & (h == 1), 0, BT)
                s = jnp.where(row <= col + near, s, -jnp.inf)
            m_old = ml_ref[0, pl.ds(h, 1), at]
            m_new = jnp.maximum(m_old, jnp.max(s, axis=0, keepdims=True))
            alpha = jnp.exp2(m_old - m_new)
            p = jnp.exp2(s - m_new)
            ml_ref[0, pl.ds(h, 1), at] = m_new
            ml_ref[1, pl.ds(h, 1), at] = ml_ref[1, pl.ds(h, 1), at] * alpha + jnp.sum(p, axis=0, keepdims=True)
            acc_ref[h, :, at] = acc_ref[h, :, at] * alpha + lax.dot_general(
                v, p.astype(BF16), (((0,), (0,)), ((), ())), preferred_element_type=F32
            )

    def visit(masked, e, carry):
        @pl.when(flags[2 * (base + e)] + flags[2 * (base + e) + 1] > 0)
        def _():
            pltpu.make_async_copy(arrays[0].at[pl.ds(0, KV)], buf.at[e], sems.at[e]).wait()

            def one(h, c2):
                @pl.when(flags[2 * (base + e) + h] > 0)
                def _():
                    unit(e, h, masked)

                return c2

            lax.fori_loop(0, 2, one, 0)

        return carry

    walk(visit, n, diag)
    if last:
        lse_ref[...] = ml_ref[0] + jnp.log2(ml_ref[1])
        for h, ref in ((0, own_ref), (1, sib_ref)):
            ref[...] = jnp.transpose(acc_ref[h] / ml_ref[1, h : h + 1, :]).astype(BF16)


def fwd_call(flags, base, q2, state, arrays, plan, diag=0, last=False):
    n = len(plan)
    first = state is None
    shapes = ((2, 2, BT), (2, HEAD_SIZE, BT))
    scratch = [pltpu.VMEM((n, KV, HEAD_SIZE), BF16), pltpu.SemaphoreType.DMA((n,))]
    if last:
        out_shape = (
            jax.ShapeDtypeStruct((BT, HEAD_SIZE), BF16),
            jax.ShapeDtypeStruct((BT, HEAD_SIZE), BF16),
            jax.ShapeDtypeStruct((2, BT), F32),
        )
        scratch = [pltpu.VMEM(shape, F32) for shape in shapes] + scratch
    else:
        out_shape = tuple(jax.ShapeDtypeStruct(shape, F32) for shape in shapes)
    return pl.pallas_call(
        functools.partial(fwd_body, base, plan, diag, first, last),
        out_shape=out_shape,
        in_specs=[SM, VM] + ([] if first else [VM] * 2) + [ANY] * len(arrays),
        out_specs=tuple(VM for _ in out_shape),
        scratch_shapes=scratch,
        name="fwd",
        cost_estimate=pl.CostEstimate(flops=n * 268435456, transcendentals=n * 524288, bytes_accessed=n * 262144),
    )(flags, q2, *(() if first else state), *arrays)


def bwd_body(base, plan, diag, first, last, *refs):
    n = len(plan)
    half = n // 2
    count = 1 + max(i for i, _ in plan)
    flags, q_ref, do_own, do_sib, lse_ref = refs[:5]
    if first:
        own_ref, sib_ref = refs[5:7]
    else:
        dq_in, delta_in = refs[5:7]
    pos = 7
    arrays = refs[pos : pos + count]
    pos += count
    if last:
        dq_own, dq_sib = refs[pos : pos + 2]
        pos += 2
    else:
        dq_out, delta_out = refs[pos : pos + 2]
        pos += 2
    keep_ref, give_ref = refs[pos : pos + 2]
    pos += 2
    dq, delta_ref, do_ref, dkv, buf, obuf, sems, osems = refs[pos : pos + 8]
    fetch(flags, base, [(arrays[i], row) for i, row in plan], buf, sems)
    do_ref[0] = do_own[...]
    do_ref[1] = do_sib[...]
    if first:
        dq[...] = jnp.zeros(dq.shape, F32)
        for h, ref in ((0, own_ref), (1, sib_ref)):
            prod = do_ref[h].astype(F32) * ref[...].astype(F32)
            delta_ref[h : h + 1, :] = jnp.sum(jnp.transpose(prod), axis=0, keepdims=True)
    else:
        dq[...] = dq_in[...]
        delta_ref[...] = delta_in[...]

    def unit(e, h, masked):
        q = q_ref[h]
        do = do_ref[h]
        lse = lse_ref[pl.ds(h, 1), :]
        delta = delta_ref[pl.ds(h, 1), :]
        for r in range(0, BT, ROWS):
            at = slice(r, r + ROWS)
            vt = slice(BT + r, BT + r + ROWS)
            k = buf[e, at, :]
            p = jnp.exp2(dot_t(k, q) * C2 - lse)
            if masked:
                row = lax.broadcasted_iota(jnp.int32, (ROWS, BT), 0) + r
                col = lax.broadcasted_iota(jnp.int32, (ROWS, BT), 1)
                near = jnp.where((e == 0) & (h == 0) | (e == diag) & (h == 1), 0, BT)
                p = jnp.where(row <= col + near, p, 0.0)
            ds = (p * (dot_t(buf[e, vt, :], do) - delta) * SCALE).astype(BF16)
            dkv[vt, :] += jnp.dot(p.astype(BF16), do, preferred_element_type=F32)
            dkv[at, :] += jnp.dot(ds, q, preferred_element_type=F32)
            dq[h] += lax.dot_general(k, ds, (((0,), (0,)), ((), ())), preferred_element_type=F32)

    def visit(masked, e, carry):
        on = flags[2 * (base + e)] + flags[2 * (base + e) + 1] > 0

        @pl.when(on)
        def _():
            pltpu.make_async_copy(arrays[0].at[pl.ds(0, KV)], buf.at[e], sems.at[e]).wait()
            dkv[...] = jnp.zeros(dkv.shape, F32)

            def one(h, c2):
                @pl.when(flags[2 * (base + e) + h] > 0)
                def _():
                    unit(e, h, masked)

                return c2

            lax.fori_loop(0, 2, one, 0)
            obuf[e] = dkv[...].astype(BF16)

        @pl.when(jnp.logical_not(on))
        def _():
            obuf[e] = jnp.zeros((KV, HEAD_SIZE), BF16)

        @pl.when(e < half)
        def _():
            pltpu.make_async_copy(obuf.at[e], keep_ref.at[pl.ds(e * KV, KV)], osems.at[e]).start()

        @pl.when(e >= half)
        def _():
            pltpu.make_async_copy(obuf.at[e], give_ref.at[pl.ds((e - half) * KV, KV)], osems.at[e]).start()

        return carry

    walk(visit, n, diag)
    if last:
        dq_own[...] = jnp.transpose(dq[0])
        dq_sib[...] = jnp.transpose(dq[1])
    else:
        dq_out[...] = dq[...]
        delta_out[...] = delta_ref[...]
    for e in range(n):
        pltpu.make_async_copy(obuf.at[e], keep_ref.at[pl.ds(0, KV)], osems.at[e]).wait()


def bwd_call(flags, base, q2, do_own, do_sib, lse, state, arrays, plan, diag=0, first=False, last=False):
    n = len(plan)
    dq_shape = (2, HEAD_SIZE, BT)
    head = jax.ShapeDtypeStruct((BT, HEAD_SIZE), F32)
    dq_outs = (head, head) if last else (jax.ShapeDtypeStruct(dq_shape, F32), jax.ShapeDtypeStruct((2, BT), F32))
    part = jax.ShapeDtypeStruct((n // 2 * KV, HEAD_SIZE), BF16)
    return pl.pallas_call(
        functools.partial(bwd_body, base, plan, diag, first, last),
        out_shape=dq_outs + (part, part),
        in_specs=[SM] + [VM] * 6 + [ANY] * len(arrays),
        out_specs=(VM,) * len(dq_outs) + (ANY, ANY),
        scratch_shapes=[
            pltpu.VMEM(dq_shape, F32),
            pltpu.VMEM((2, BT), F32),
            pltpu.VMEM((2, BT, HEAD_SIZE), BF16),
            pltpu.VMEM((KV, HEAD_SIZE), F32),
            pltpu.VMEM((n, KV, HEAD_SIZE), BF16),
            pltpu.VMEM((n, KV, HEAD_SIZE), BF16),
            pltpu.SemaphoreType.DMA((n,)),
            pltpu.SemaphoreType.DMA((n,)),
        ],
        name="bwd",
        cost_estimate=pl.CostEstimate(flops=n * 671088640, transcendentals=n * 524288, bytes_accessed=n * 524288),
    )(flags, q2, do_own, do_sib, lse, *state, *arrays)


def grads_body(where_ref, a_ref, *refs):
    pieces, weights = refs[:4], refs[4:8]
    keep_ref, give_ref, mine_ref, other_ref, at, acc = refs[8:]
    step = pl.program_id(0)

    @pl.when(step == 0)
    def _():
        at[...] = jnp.transpose(a_ref[...])
        acc[...] = jnp.zeros(acc.shape, F32)

    first = where_ref[2] == 0
    total = acc[...]
    for i in range(4):
        piece = pieces[i][...]
        total = total + dot_t(piece, weights[i][...])
        term = jnp.dot(at[...], piece, preferred_element_type=F32).astype(BF16)
        keep_ref[i] = jnp.where(first, term[:, :128], term[:, 128:])
        give_ref[i] = jnp.where(first, term[:, 128:], term[:, :128])
    acc[...] = total

    @pl.when(step == pl.num_programs(0) - 1)
    def _():
        low = total.astype(BF16)
        mine_ref[...] = jnp.where(first, low[:, :128], low[:, 128:])
        other_ref[...] = jnp.where(first, low[:, 128:], low[:, :128])


def grads_call(where, attn, piece, w_out):
    rows, width = attn.shape

    def column(i):
        return lambda p, w: (0, 4 * (w[0] ^ (p % 2 + i // 2 * 2)) + (w[1] ^ (p // 2 + i % 2 * 2)))

    out = jax.ShapeDtypeStruct((16, width, 128), BF16)
    spec = pl.BlockSpec((4, width, 128), lambda p, w: (p, 0, 0))
    return pl.pallas_call(
        grads_body,
        grid_spec=pltpu.PrefetchScalarGridSpec(
            num_scalar_prefetch=1,
            grid=(4,),
            in_specs=[pl.BlockSpec((rows, width), lambda p, w: (0, 0))]
            + [pl.BlockSpec((rows, 256), column(i)) for i in range(4)]
            + [pl.BlockSpec((width, 256), column(i)) for i in range(4)],
            out_specs=[spec, spec] + [pl.BlockSpec((rows, HEAD_SIZE), lambda p, w: (0, 0))] * 2,
            scratch_shapes=[pltpu.VMEM((width, rows), BF16), pltpu.VMEM((rows, width), F32)],
        ),
        out_shape=(out, out) + (jax.ShapeDtypeStruct((rows, HEAD_SIZE), BF16),) * 2,
        name="grads",
        cost_estimate=pl.CostEstimate(flops=2147483648, transcendentals=0, bytes_accessed=8912896),
    )(where, attn, *([piece] * 4), *([w_out] * 4))


def send(value, rule):
    pairs = []
    for b in range(NB):
        to = rule(b // 8, b // 2 % 4, b % 2)
        if to is not None:
            x, y, c = to
            pairs.append((b, 8 * x + 2 * y + c))
    return lax.ppermute(value, "ctx", pairs)


def swap(value):
    return send(value, lambda x, y, c: (x, y, 1 - c))


def ahead(value):
    return send(value, lambda x, y, c: (x + 1, y, c) if x < 3 else None)


def back(value):
    return send(value, lambda x, y, c: (x - 1, y, c) if x > 0 else None)


def along(value, k):
    return send(value, lambda x, y, c: (x, (y + k) % 4, c))


def bf(v):
    return v.astype(BF16)


def f32(v):
    return v.astype(F32)


def per_device(query_proj, projected_keys, projected_values, w_out, attended_blocks, grad_out):
    rank = lax.axis_index("ctx")
    x, y, c = rank // 8, rank // 2 % 4, rank % 2
    sib = rank + 1 - 2 * c

    piece = lax.all_gather(grad_out, "head", axis=1, tiled=True)

    def mine_of(v):
        return jnp.where(c == 0, v[:, :HEAD_SIZE], v[:, HEAD_SIZE:])

    def other_of(v):
        return jnp.where(c == 0, v[:, HEAD_SIZE:], v[:, :HEAD_SIZE])

    def joined(own, other):
        return jnp.where(c == 0, jnp.concatenate([own, other], 1), jnp.concatenate([other, own], 1))

    own = jnp.concatenate([projected_keys, projected_values], 0)
    x1 = ahead(own)
    ownx = swap(jnp.concatenate([projected_keys, projected_values, other_of(query_proj)], 0))
    d1 = along(jnp.where(y < 3, own, x1), 1)
    d2 = along(jnp.where(y < 2, own, x1), 2)
    d3 = along(jnp.where(y < 1, own, x1), 3)
    d8 = ahead(x1)
    x1x = swap(x1)
    pre = jnp.concatenate([d1, d2], 0)
    far = ahead(pre)
    prex = swap(pre)
    d3x = swap(d3)
    d8x = swap(d8)
    farx = swap(far)
    q2 = jnp.stack([mine_of(query_proj), ownx[KV:]])

    keys = jnp.concatenate([b - 2 * jnp.array(d) for d in ([0], [1, 2, 4, 3], [5, 6, 8], [0, 1, 2, 4, 3]) for b in (rank, sib)])
    lists = jnp.stack(
        [lax.dynamic_index_in_dim(attended_blocks, r, 0, keepdims=False) for r in (rank, sib)]
    )
    hit = jnp.any(lists[None] == keys[:, None, None], -1) & (keys >= 0)[:, None]
    flags = hit.astype(jnp.int32).reshape(-1)
    self_blocks = ([own, ownx], ((0, 0), (1, 0)))
    near_blocks = ([pre, x1, d3, prex, x1x, d3x], ((0, 0), (0, KV), (1, 0), (2, 0), (3, 0), (3, KV), (4, 0), (5, 0)))
    far_blocks = ([far, d8, farx, d8x], ((0, 0), (0, KV), (1, 0), (2, 0), (2, KV), (3, 0)))
    all_blocks = ([own, ownx] + near_blocks[0], ((0, 0), (2, 0), (2, KV), (3, 0), (4, 0), (1, 0), (5, 0), (5, KV), (6, 0), (7, 0)))
    state = fwd_call(flags, 0, q2, None, *self_blocks, diag=1)
    state = fwd_call(flags, 2, q2, state, *near_blocks)
    attn_own, attn_sib, lse = fwd_call(flags, 10, q2, state, *far_blocks, last=True)
    attn_other = swap(attn_sib)
    attn = joined(attn_own, attn_other)

    out_terms = bf(jnp.dot(attn, w_out, preferred_element_type=F32))
    layer_out = lax.psum_scatter(out_terms, "head", scatter_dimension=1, tiled=True)
    wkeep, wgive, do_own, do_other = grads_call(jnp.stack([x, y, c]), attn, piece, w_out)
    do_sib = swap(do_other)
    wcame = swap(wgive)

    def summed(n, parts, sent):
        low, high = [p[:n] for p in parts] + [sent[:n]], [p[n : 2 * n] for p in parts] + [sent[n : 2 * n]]
        return low, bf(sum(f32(p) for p in high))

    args = (q2, do_own, do_sib, lse)
    dq, delta, keep, give = bwd_call(flags, 10, *args, (attn_own, attn_sib), *far_blocks, first=True)
    got = swap(give)
    came = back(bf(f32(keep) + f32(got)))
    parts, gave = summed(8, [wkeep], wcame)
    wcame = send(gave, lambda x, y, c: (x, y ^ 1, c))
    dq_own, dq_sib, keep, give = bwd_call(flags, 16, *args, (dq, delta), *all_blocks, diag=5, last=True)
    got = swap(give)
    dq_other = swap(dq_sib)
    parts, gave = summed(4, parts, wcame)
    wcame = send(gave, lambda x, y, c: (x ^ 1, y, c))
    t0, t1, t2, t4, t3 = [f32(keep[at]) + f32(got[at]) for at in (slice(i * KV, (i + 1) * KV) for i in range(5))]
    t1, t2, t4 = [t + f32(came[i * KV : (i + 1) * KV]) for i, t in enumerate((t1, t2, t4))]
    s1 = along(bf(t1), -1)
    s2 = along(bf(t2), -2)
    s3 = along(bf(t3), -3)
    parts, gave = summed(2, parts, wcame)
    wcame = send(gave, lambda x, y, c: (x ^ 2, y, c))

    def kept(cond, v):
        return jnp.where(cond, f32(v), 0.0)

    r4 = back(bf(t4 + kept(y == 3, s1) + kept(y >= 2, s2) + kept(y >= 1, s3)))
    parts, gave = summed(1, parts, wcame)
    gave, part = lax.optimization_barrier((gave, sum(f32(p[0]) for p in parts)))
    wcame = send(gave, lambda x, y, c: (x, y ^ 2, c))
    grad_wout = part + f32(wcame[0])
    grad_query = joined(dq_own, dq_other)
    total = t0 + kept(y < 3, s1) + kept(y < 2, s2) + kept(y < 1, s3)
    total = lax.optimization_barrier(total)
    grad_key, grad_value = [total[at] + f32(r4[at]) for at in (slice(0, BT), slice(BT, KV))]
    return (layer_out, grad_query, grad_key, grad_value, grad_wout)


def solution(mesh):
    return jax.shard_map(
        per_device,
        mesh=mesh,
        in_specs=(
            P("ctx", "head"),
            P("ctx", "head"),
            P("ctx", "head"),
            P("head", None),
            P(),
            P("ctx", "head"),
        ),
        out_specs=(
            P("ctx", "head"),
            P("ctx", "head"),
            P("ctx", "head"),
            P("ctx", "head"),
            P("head", "ctx"),
        ),
        check_vma=False,
    )
```
